32 devices in a mesh: col: 8 (over y, x, core), row: 4 (over z).
Axes of the slice: x: 2, y: 2, z: 4, core: 2. Of those that a mesh axis runs over, the one named last changes fastest.
Arguments:
- matrix: float32 [16, 512, 4096], P(None, 'row', 'col'), may hold values from -0.4 to 2.4, as said below
- pivots: int32 [8, 512], replicated, may hold values from 0 to 511, as said below
- seeds: float32 [8, 512, 512], P('col'), may hold values from -1 to 2, as said below
Outputs:
- factors: float32 [16, 512, 4096], P(None, 'row', 'col')
The draws below stay inside these ranges and needn't reach their ends.
Inputs may be any that keep to these rules, and one draw needn't show every extreme that they name: Each row of pivots is an ordering of 0 .. 511. Block (r, j) of matrix is zero where r and j differ by more than 8. seeds[k] approximates the inverse of block (k, k) of matrix after the replacement of rows by pivots[k].
All inputs are finite; a program needn't handle non-finite values.
Results may differ from the reference program's by a relative error of at most 0.0001.
Values sent between devices are 32-bit elements; how exact they have to be, the bound alone decides.
A program may use at most 64 MiB of HBM per device.

```python
import math
import jax
import jax.numpy as jnp
from jax import lax

B = 512
HB = 8
SWEEPS = 2
PANELS = 8
NBLK = 16
COLS = 4096


def build_all(key):
    key_perm, key_vals, key_diag, key_noise = jax.random.split(jax.random.fold_in(key, 4242), 4)
    pivots = jax.vmap(lambda one_key: jax.random.permutation(one_key, B))(jax.random.split(key_perm, PANELS)).astype(jnp.int32)
    values = jnp.clip(jax.random.normal(key_vals, (NBLK, B, COLS), jnp.float32), -4.0, 4.0)
    block_rows = jnp.arange(NBLK)[:, None, None]
    block_cols = (jnp.arange(COLS) // B)[None, None, :]
    offset = block_rows - block_cols
    spread = jnp.where(offset == 0, 0.35, 0.165) / math.sqrt(B)
    spread = jnp.where(jnp.abs(offset) <= HB, spread, 0.0)
    diag_values = jnp.exp(jax.random.uniform(key_diag, (NBLK, B), jnp.float32, 0.0, math.log(2.0)))
    on_diagonal = (jnp.arange(B)[None, :, None] == (jnp.arange(COLS) % B)[None, None, :]) & (offset == 0)
    permuted = values * spread + jnp.where(on_diagonal, diag_values[:, :, None], 0.0)
    leading = permuted[:PANELS].reshape(PANELS, B, PANELS, B)
    diag_blocks = leading[jnp.arange(PANELS), :, jnp.arange(PANELS), :]
    identity = jnp.eye(B, dtype=jnp.float32)
    approx = identity[None] / diag_values[:PANELS, None, :]
    for sweep_index in range(12):
        product = jnp.einsum('pij,pjk->pik', diag_blocks, approx, precision=lax.Precision.HIGHEST)
        approx = jnp.einsum('pij,pjk->pik', approx, 2.0 * identity[None] - product, precision=lax.Precision.HIGHEST)
    noise = jnp.clip(jax.random.normal(key_noise, (PANELS, B, B), jnp.float32), -4.0, 4.0) * (0.25 / math.sqrt(B))
    seeds = approx - jnp.einsum('pij,pjk->pik', approx, noise, precision=lax.Precision.HIGHEST)
    inverse_order = jnp.argsort(pivots, axis=1).astype(jnp.int32)
    top_rows = jnp.take_along_axis(permuted[:PANELS], inverse_order[:, :, None], axis=1)
    matrix = jnp.concatenate([top_rows, permuted[PANELS:]], axis=0)
    return (matrix, pivots, seeds)


def draw_matrix(key, part):
    return build_all(key)[0]


def draw_pivots(key, part):
    return build_all(key)[1]


def draw_seeds(key, part):
    return build_all(key)[2]


def setup_inputs(seed: int = 0) -> dict:
    key_list = jax.random.split(jax.random.key(seed), 4)
    return {
        "matrix": draw_matrix(jax.random.fold_in(key_list[3], 71), 0),
        "pivots": draw_pivots(jax.random.fold_in(key_list[3], 71), 0),
        "seeds": draw_seeds(jax.random.fold_in(key_list[3], 71), 0),
    }


def dot_high(left, right):
    return jnp.dot(left, right, precision=lax.Precision.HIGHEST, preferred_element_type=jnp.float32)


def reference(matrix, pivots, seeds):
    factors = matrix
    identity = jnp.eye(B, dtype=jnp.float32)
    column_ids = jnp.arange(COLS)
    for panel_index in range(PANELS):
        panel_cols = slice(panel_index * B, (panel_index + 1) * B)
        row_block = factors[panel_index]
        swapped = jnp.take(row_block, pivots[panel_index], axis=0)
        col_mask = (column_ids >= panel_index * B)[None, :]
        row_block = jnp.where(col_mask, swapped, row_block)
        factors = factors.at[panel_index].set(row_block)
        pivot_block = row_block[:, panel_cols]
        approx = seeds[panel_index]
        for sweep_index in range(SWEEPS):
            approx = dot_high(approx, 2.0 * identity - dot_high(pivot_block, approx))
        below_rows = factors[panel_index + 1:panel_index + HB + 1, :, panel_cols].reshape(HB * B, B)
        multipliers = dot_high(below_rows, approx)
        factors = factors.at[panel_index + 1:panel_index + HB + 1, :, panel_cols].set(multipliers.reshape(HB, B, B))
        last_panel = min(panel_index + HB, PANELS - 1)
        if last_panel >= panel_index + 1:
            trail_cols = slice((panel_index + 1) * B, (last_panel + 1) * B)
            upper_rows = row_block[:, trail_cols]
            change = dot_high(multipliers, upper_rows).reshape(HB, B, -1)
            factors = factors.at[panel_index + 1:panel_index + HB + 1, :, trail_cols].add(-change)
    return factors
```

```python
import functools

import jax
import jax.numpy as jnp
from jax import lax
from jax.experimental import pallas as pl
from jax.experimental.pallas import tpu as pltpu
from jax.sharding import PartitionSpec as P

HB = 8
SWEEPS = 2
F32 = jnp.float32
BF16 = jnp.bfloat16
MESH = pl.DeviceIdType.MESH


def split(x):
    high = x.astype(BF16)
    return high, (x - high.astype(F32)).astype(BF16)


def dot(left, right):
    return jnp.dot(left, right, preferred_element_type=F32)


def dot3(left, right):
    return dot(left[0], right[0]) + (dot(left[0], right[1]) + dot(left[1], right[0]))


def split3(x):
    high, rest = split(x)
    middle = rest
    return high, middle, (x - high.astype(F32) - middle.astype(F32)).astype(BF16)


def kernel(
    ncol, nrow, a_hbm, pivc_ref, pivr_ref, seed_ref, out_ref,
    upper, mult, u_high, u_low, approx, y_high, y_low,
    usend, urecv, msend, mrecv, lsem,
):
    col = lax.axis_index("col")
    row = lax.axis_index("row")
    right = lax.rem(col + 1, ncol)
    left = lax.rem(col + ncol - 1, ncol)
    share, width = out_ref.shape[1], out_ref.shape[2]
    first = jnp.maximum(col - HB, 0)

    load = pltpu.make_async_copy(a_hbm, out_ref, lsem)
    load.start()
    barrier = pltpu.get_barrier_semaphore()
    for step in range(1, nrow):
        pl.semaphore_signal(
            barrier, inc=1, device_id=(col, lax.rem(row + step, nrow)), device_id_type=MESH
        )
    for side in (left, right):
        pl.semaphore_signal(barrier, inc=1, device_id=(side, row), device_id_type=MESH)
    pl.semaphore_wait(barrier, nrow + 1)
    load.wait()

    def share_copy(k, step, source, target):
        return pltpu.make_async_remote_copy(
            src_ref=upper.at[k, source],
            dst_ref=upper.at[k, source],
            send_sem=usend.at[k, step],
            recv_sem=urecv.at[k, source],
            device_id=(col, target),
            device_id_type=MESH,
        )

    def start_gather(k):
        upper[k, row] = out_ref[k]
        for step in range(1, nrow):
            share_copy(k, step, row, lax.rem(row + step, nrow)).start()

    def finish_gather(k):
        for step in range(1, nrow):
            source = lax.rem(row + step, nrow)
            share_copy(k, step, source, source).wait_recv()

    def mult_copy(k, c):
        return pltpu.make_async_remote_copy(
            src_ref=mult.at[k, c],
            dst_ref=mult.at[k, c],
            send_sem=msend.at[k, c],
            recv_sem=mrecv.at[k, c],
            device_id=(right, row),
            device_id_type=MESH,
        )

    def store_swapped(k):
        picks = lax.broadcasted_iota(jnp.int32, (share, width), 1) == pivc_ref[k]
        picks = jnp.where(picks, 1.0, 0.0).astype(BF16)
        parts = split3(upper[k].reshape(width, width))
        out_ref[k] = dot(picks, parts[0]) + (dot(picks, parts[1]) + dot(picks, parts[2]))

    def split_upper(k):
        high, low = split(upper[k].reshape(width, width))
        u_high[...] = high
        u_low[...] = low

    start_gather(first)

    ordering = jnp.broadcast_to(pivr_ref[col], (width, width))
    scatter = lax.broadcasted_iota(jnp.int32, (width, width), 0) == ordering
    scatter = jnp.where(scatter, 1.0, 0.0).astype(BF16)
    seed_parts = split3(seed_ref[0])
    contract = (((1,), (1,)), ((), ()))
    total = lax.dot_general(seed_parts[2], scatter, contract, preferred_element_type=F32)
    total += lax.dot_general(seed_parts[1], scatter, contract, preferred_element_type=F32)
    total += lax.dot_general(seed_parts[0], scatter, contract, preferred_element_type=F32)
    approx[...] = total

    def update(k, carry):
        finish_gather(k)
        split_upper(k)
        store_swapped(k)
        passes_on = (col + 1 < ncol) & (col + 1 <= k + HB)

        def chunk(c):
            copy = mult_copy(k, c)
            copy.wait_recv()

            @pl.when(passes_on)
            def _():
                copy.start()

            change = dot3(split(mult[k, c]), (u_high[...], u_low[...]))
            out_ref[k + 1 + c] = out_ref[k + 1 + c] - change

        chunk(0)
        start_gather(k + 1)

        @pl.loop(1, HB)
        def _(c):
            chunk(c)

        return carry

    lax.fori_loop(first, col, update, 0)

    finish_gather(col)
    split_upper(col)
    diagonal = lax.broadcasted_iota(jnp.int32, (width, width), 0)
    diagonal = diagonal == lax.broadcasted_iota(jnp.int32, (width, width), 1)

    @pl.loop(0, SWEEPS)
    def _(sweep):
        parts = split(approx[...])
        product = dot3((u_high[...], u_low[...]), parts)
        approx[...] = dot3(parts, split(jnp.where(diagonal, 2.0, 0.0) - product))

    high, low = split(approx[...])
    y_high[...] = high
    y_low[...] = low

    @pl.loop(0, HB)
    def _(c):
        mult[col, c] = dot3(split(out_ref[col + 1 + c]), (y_high[...], y_low[...]))

        @pl.when(col + 1 < ncol)
        def _():
            mult_copy(col, c).start()

    store_swapped(col)
    y_high[...] = scatter

    @pl.loop(0, HB)
    def _(c):
        parts = split3(mult[col, c])
        target = y_high[...]
        out_ref[col + 1 + c] = dot(parts[0], target) + (dot(parts[1], target) + dot(parts[2], target))

    def drain(k, carry):
        for step in range(1, nrow):
            share_copy(k, step, row, lax.rem(row + step, nrow)).wait_send()

        @pl.when((col + 1 < ncol) & (col + 1 <= k + HB))
        def _():
            @pl.loop(0, HB)
            def _(c):
                mult_copy(k, c).wait_send()

        return carry

    lax.fori_loop(first, col + 1, drain, 0)


def local(matrix, pivots, seeds):
    ncol = lax.axis_size("col")
    nrow = lax.axis_size("row")
    nblk, share, width = matrix.shape
    start = lax.axis_index("row") * share
    by_row = lax.dynamic_slice_in_dim(pivots, start, share, 1)[:, :, None]
    by_col = pivots[:, None, :]
    vmem = pl.BlockSpec(memory_space=pltpu.VMEM)
    return pl.pallas_call(
        functools.partial(kernel, ncol, nrow),
        out_shape=jax.ShapeDtypeStruct(matrix.shape, F32),
        in_specs=[pl.BlockSpec(memory_space=pl.ANY), vmem, vmem, vmem],
        out_specs=vmem,
        scratch_shapes=[
            pltpu.VMEM((ncol, nrow, share, width), F32),
            pltpu.VMEM((ncol, HB, share, width), F32),
            pltpu.VMEM((width, width), BF16),
            pltpu.VMEM((width, width), BF16),
            pltpu.VMEM((width, width), F32),
            pltpu.VMEM((width, width), BF16),
            pltpu.VMEM((width, width), BF16),
            pltpu.SemaphoreType.DMA((ncol, nrow)),
            pltpu.SemaphoreType.DMA((ncol, nrow)),
            pltpu.SemaphoreType.DMA((ncol, HB)),
            pltpu.SemaphoreType.DMA((ncol, HB)),
            pltpu.SemaphoreType.DMA,
        ],
        compiler_params=pltpu.CompilerParams(
            collective_id=0, has_side_effects=True, vmem_limit_bytes=60 * 1024 * 1024
        ),
    )(matrix, by_row, by_col, seeds)


def solution(mesh):
    return jax.shard_map(
        local,
        mesh=mesh,
        in_specs=(P(None, "row", "col"), P(), P("col", None, None)),
        out_specs=P(None, "row", "col"),
        check_vma=False,
    )
```

```python
import functools

import jax
import jax.numpy as jnp
from jax import lax
from jax.experimental import pallas as pl
from jax.experimental.pallas import tpu as pltpu
from jax.sharding import PartitionSpec as P

HB = 8
SWEEPS = 2
CHIPS = 4
F32 = jnp.float32
BF16 = jnp.bfloat16
MESH = pl.DeviceIdType.MESH


def split(x):
    high = x.astype(BF16)
    return high, (x - high.astype(F32)).astype(BF16)


def dot(left, right):
    return jnp.dot(left, right, preferred_element_type=F32)


def dot3(left, right):
    return dot(left[0], right[0]) + (dot(left[0], right[1]) + dot(left[1], right[0]))


def split3(x):
    high, rest = split(x)
    middle = rest
    return high, middle, (x - high.astype(F32) - middle.astype(F32)).astype(BF16)


def kernel(
    ncol, nrow, a_hbm, pivc_ref, pivr_ref, seed_ref, out_ref,
    upper, mult, u_high, u_low, approx, y_high, y_low,
    usend, urecv, msend, mrecv, lsem,
):
    col = lax.axis_index("col")
    row = lax.axis_index("row")
    share, width = out_ref.shape[1], out_ref.shape[2]
    first = jnp.maximum(col - HB, 0)

    load = pltpu.make_async_copy(a_hbm, out_ref, lsem)
    load.start()
    barrier = pltpu.get_barrier_semaphore()
    for step in range(1, nrow):
        pl.semaphore_signal(
            barrier, inc=1, device_id=(col, lax.rem(row + step, nrow)), device_id_type=MESH
        )
    for step in range(1, ncol):
        pl.semaphore_signal(
            barrier, inc=1, device_id=(lax.rem(col + step, ncol), row), device_id_type=MESH
        )
    pl.semaphore_wait(barrier, nrow + ncol - 2)
    load.wait()

    def share_copy(k, step, source, target):
        return pltpu.make_async_remote_copy(
            src_ref=upper.at[k, source],
            dst_ref=upper.at[k, source],
            send_sem=usend.at[k, step],
            recv_sem=urecv.at[k, source],
            device_id=(col, target),
            device_id_type=MESH,
        )

    def start_gather(k):
        upper[k, row] = out_ref[k]
        for step in range(1, nrow):
            share_copy(k, step, row, lax.rem(row + step, nrow)).start()

    def finish_gather(k):
        for step in range(1, nrow):
            source = lax.rem(row + step, nrow)
            share_copy(k, step, source, source).wait_recv()

    paired = ncol == 2 * CHIPS and ncol <= HB + 1

    def mult_copy(k, c, way, target):
        return pltpu.make_async_remote_copy(
            src_ref=mult.at[k, c],
            dst_ref=mult.at[k, c],
            send_sem=msend.at[k, c, way],
            recv_sem=mrecv.at[k, c],
            device_id=(target, row),
            device_id_type=MESH,
        )

    def routes(k, path):
        if not paired:
            return [((col + 1 < ncol) & (col + 1 <= k + HB), lax.rem(col + 1, ncol))]
        chip, core, owner = col // 2, col % 2, k // 2
        at_owner = col == k
        carries = at_owner | ((chip > owner) & (core == path))
        beside = (at_owner & (core == 0)) | ((chip > owner) & (core == path))
        if path == 0:
            onward = [(chip == 0, 1), (chip == 1, 3), ((chip == 3) & (owner < 2), 2),
                      ((chip == 2) & (owner == 2), 3)]
        else:
            onward = [(chip == 0, 2), ((chip == 1) & (owner == 1), 2), (chip == 2, 3),
                      ((chip == 3) & (owner == 0), 1)]
        found = onward[0][0]
        target = 0
        for test, goal in onward:
            found = found | test
            target = target + jnp.where(test, goal, 0)
        away = lax.rem(2 * target + path, ncol)
        return [(carries & found, away), (beside, chip * 2 + 1 - core)]

    def pass_on(k, c, path):
        for way, (test, target) in enumerate(routes(k, path)):
            @pl.when(test)
            def _():
                mult_copy(k, c, way, target).start()

    def drain_sends(k, c, path):
        for way, (test, target) in enumerate(routes(k, path)):
            @pl.when(test)
            def _():
                mult_copy(k, c, way, target).wait_send()

    def store_swapped(k):
        picks = lax.broadcasted_iota(jnp.int32, (share, width), 1) == pivc_ref[k]
        picks = jnp.where(picks, 1.0, 0.0).astype(BF16)
        parts = split3(upper[k].reshape(width, width))
        out_ref[k] = dot(picks, parts[0]) + (dot(picks, parts[1]) + dot(picks, parts[2]))

    def split_upper(k):
        high, low = split(upper[k].reshape(width, width))
        u_high[...] = high
        u_low[...] = low

    start_gather(first)

    ordering = jnp.broadcast_to(pivr_ref[col], (width, width))
    scatter = lax.broadcasted_iota(jnp.int32, (width, width), 0) == ordering
    scatter = jnp.where(scatter, 1.0, 0.0).astype(BF16)
    seed_parts = split3(seed_ref[0])
    contract = (((1,), (1,)), ((), ()))
    total = lax.dot_general(seed_parts[2], scatter, contract, preferred_element_type=F32)
    total += lax.dot_general(seed_parts[1], scatter, contract, preferred_element_type=F32)
    total += lax.dot_general(seed_parts[0], scatter, contract, preferred_element_type=F32)
    approx[...] = total

    def update(k, carry):
        finish_gather(k)
        split_upper(k)
        store_swapped(k)

        def chunk(c, path):
            mult_copy(k, c, 0, lax.rem(col + 1, ncol)).wait_recv()
            pass_on(k, c, path)
            change = dot3(split(mult[k, c]), (u_high[...], u_low[...]))
            out_ref[k + 1 + c] = out_ref[k + 1 + c] - change

        later = (col == k + 2) & (col % 2 == 1) & paired
        chunk(0, 0)

        @pl.when(jnp.logical_not(later))
        def _():
            start_gather(k + 1)

        chunk(1, 1)

        @pl.loop(1, HB // 2)
        def _(c):
            chunk(2 * c, 0)
            chunk(2 * c + 1, 1)

        @pl.when(later)
        def _():
            start_gather(k + 1)

        return carry

    lax.fori_loop(first, col, update, 0)

    finish_gather(col)
    split_upper(col)
    diagonal = lax.broadcasted_iota(jnp.int32, (width, width), 0)
    diagonal = diagonal == lax.broadcasted_iota(jnp.int32, (width, width), 1)

    @pl.loop(0, SWEEPS)
    def _(sweep):
        parts = split(approx[...])
        product = dot3((u_high[...], u_low[...]), parts)
        approx[...] = dot3(parts, split(jnp.where(diagonal, 2.0, 0.0) - product))

    high, low = split(approx[...])
    y_high[...] = high
    y_low[...] = low

    @pl.loop(0, HB // 2)
    def _(pair):
        for path in range(2):
            c = 2 * pair + path
            mult[col, c] = dot3(split(out_ref[col + 1 + c]), (y_high[...], y_low[...]))
            pass_on(col, c, path)

    store_swapped(col)
    y_high[...] = scatter

    @pl.loop(0, HB)
    def _(c):
        parts = split3(mult[col, c])
        target = y_high[...]
        out_ref[col + 1 + c] = dot(parts[0], target) + (dot(parts[1], target) + dot(parts[2], target))

    def drain(k, carry):
        for step in range(1, nrow):
            share_copy(k, step, row, lax.rem(row + step, nrow)).wait_send()

        @pl.loop(0, HB // 2)
        def _(pair):
            for path in range(2):
                drain_sends(k, 2 * pair + path, path)

        return carry

    lax.fori_loop(first, col + 1, drain, 0)


def local(matrix, pivots, seeds):
    ncol = lax.axis_size("col")
    nrow = lax.axis_size("row")
    nblk, share, width = matrix.shape
    start = lax.axis_index("row") * share
    by_row = lax.dynamic_slice_in_dim(pivots, start, share, 1)[:, :, None]
    by_col = pivots[:, None, :]
    vmem = pl.BlockSpec(memory_space=pltpu.VMEM)
    return pl.pallas_call(
        functools.partial(kernel, ncol, nrow),
        out_shape=jax.ShapeDtypeStruct(matrix.shape, F32),
        in_specs=[pl.BlockSpec(memory_space=pl.ANY), vmem, vmem, vmem],
        out_specs=vmem,
        scratch_shapes=[
            pltpu.VMEM((ncol, nrow, share, width), F32),
            pltpu.VMEM((ncol, HB, share, width), F32),
            pltpu.VMEM((width, width), BF16),
            pltpu.VMEM((width, width), BF16),
            pltpu.VMEM((width, width), F32),
            pltpu.VMEM((width, width), BF16),
            pltpu.VMEM((width, width), BF16),
            pltpu.SemaphoreType.DMA((ncol, nrow)),
            pltpu.SemaphoreType.DMA((ncol, nrow)),
            pltpu.SemaphoreType.DMA((ncol, HB, 2)),
            pltpu.SemaphoreType.DMA((ncol, HB)),
            pltpu.SemaphoreType.DMA,
        ],
        compiler_params=pltpu.CompilerParams(
            collective_id=0, has_side_effects=True, vmem_limit_bytes=60 * 1024 * 1024
        ),
    )(matrix, by_row, by_col, seeds)


def solution(mesh):
    return jax.shard_map(
        local,
        mesh=mesh,
        in_specs=(P(None, "row", "col"), P(), P("col", None, None)),
        out_specs=P(None, "row", "col"),
        check_vma=False,
    )
```
